32 devices in a mesh: rep: 2 (over x), exp: 4 (over y, core), shard: 4 (over z).
Axes of the slice: x: 2, y: 2, z: 4, core: 2. Of those that a mesh axis runs over, the one named last changes fastest.
Arguments:
- deltas: bfloat16 [2, 4, 2048, 7168], P('rep', 'exp', 'shard'), may hold values from -0.1875 to 0.1875
- master: float32 [4, 2048, 7168], P('exp', 'shard', 'rep'), may hold values from -0.125 to 0.125
- momentum: float32 [4, 2048, 7168], P('exp', 'shard', 'rep'), may hold values from -0.12 to 0.12
- tokens: bfloat16 [4, 2048, 2048], P('exp', 'shard'), may hold values from -6 to 6
Outputs:
- new_master: float32 [4, 2048, 7168], P('exp', 'shard', 'rep')
- new_momentum: float32 [4, 2048, 7168], P('exp', 'shard', 'rep')
- probe_out: bfloat16 [4, 2048, 7168], P('exp', 'shard', 'rep')
The draws below stay inside these ranges and needn't reach their ends.
All inputs are finite; a program needn't handle non-finite values.
Results may differ from the reference program's by a relative error of at most 0.014.
Values may be sent and summed in bfloat16 or wider, within the bound.
A program may use at most 128 MiB of HBM per device.

```python
import jax
import jax.numpy as jnp
from jax import lax

DW = 2048
FW = 7168
EXPERTS = 4
TOKENS = 2048
N_REP = 2


def strengthened(drawn, own_key, source, target, parts, factor):
    owner, partner = [(jnp.arange(drawn.shape[axis_at]) // (drawn.shape[axis_at] // parts)).reshape([-1 if axis == axis_at else 1 for axis in range(drawn.ndim)]) for axis_at in (source, target)]
    chosen = jax.random.permutation(own_key, parts)[partner]
    strong = (owner == chosen) | (owner == (partner + parts // 2) % parts)
    return jnp.where(strong, factor * drawn, drawn)


def block_levels(rng, shape, shards, smallest, top_value):
    loudness = 1.0
    for axis_at, blocks in shards:
        steps = jax.random.uniform(jax.random.fold_in(jax.random.fold_in(rng, 6), axis_at), (blocks,), jnp.float32, smallest / len(shards), top_value / len(shards))
        loudness = loudness * jnp.repeat(jnp.exp(steps), shape[axis_at] // blocks).reshape((-1,) + (1,) * (len(shape) - 1 - axis_at))
    return loudness


def scatter_about(key, extent, deviation, most, shards=(), kind=jnp.bfloat16):
    factor_of = block_levels(key, extent, shards, -0.22, 0.18) if shards else 1.0
    values = jax.random.normal(key, extent, jnp.float32) * deviation * factor_of
    return jnp.minimum(jnp.maximum(values, -most), most).astype(kind)


def bell_draw_with(own_key, dims, spread, reach, cuts, heavy, kind=jnp.bfloat16):
    entries = spread * jax.random.normal(own_key, dims, jnp.float32)
    if cuts:
        entries = entries * block_levels(own_key, dims, cuts, -0.22, 0.18)
    return jnp.clip(strengthened(entries, jax.random.fold_in(own_key, 3), *heavy), -reach, reach).astype(kind)


def setup_inputs(seed: int = 0) -> dict:
    key_list = jax.random.split(jax.random.key(seed), 5)
    deltas = bell_draw_with(key_list[0], (N_REP, EXPERTS, DW, FW), DW ** -0.5, 0.1875, ((0, 2), (1, 4), (2, 4)), (0, 3, 2, 2.0))
    master = scatter_about(key_list[1], (EXPERTS, DW, FW), DW ** -0.5, 0.125, ((0, 4), (1, 4), (2, 2)), jnp.float32)
    momentum = scatter_about(key_list[2], (EXPERTS, DW, FW), 0.02, 0.12, ((0, 4), (1, 4), (2, 2)), jnp.float32)
    tokens = scatter_about(key_list[3], (EXPERTS, TOKENS, DW), 1.0, 6.0, ((0, 4), (1, 4)))
    return {"deltas": deltas, "master": master, "momentum": momentum, "tokens": tokens}


outer_rate = 0.7
momentum_coef = 0.9


def reference(deltas, master, momentum, tokens):
    def accumulate(running, delta_one):
        return running + delta_one.astype(jnp.float32), None

    start_sum = jnp.zeros(master.shape, jnp.float32)
    summed, unused = lax.scan(accumulate, start_sum, deltas)
    outer_grad = summed / N_REP
    new_momentum = momentum_coef * momentum + outer_grad
    new_master = master - outer_rate * (outer_grad + momentum_coef * new_momentum)
    weight_bf = new_master.astype(jnp.bfloat16)
    probe_out = jnp.einsum("etd,edf->etf", tokens.astype(jnp.float32), weight_bf.astype(jnp.float32))
    return new_master, new_momentum, probe_out.astype(jnp.bfloat16)
```

```python
import functools

import jax
import jax.numpy as jnp
from jax import lax
from jax.experimental import pallas as pl
from jax.experimental.pallas import tpu as pltpu
from jax.sharding import PartitionSpec as P

outer_rate = 0.7
momentum_coef = 0.9
MESH = pl.DeviceIdType.MESH
CHUNK = 128
AHEAD = 6
TRAIL = 3
ROWS = 256


def plain_body(deltas, master, momentum, tokens):
    summed = lax.psum_scatter(
        deltas[0, 0].astype(jnp.float32).astype(jnp.bfloat16),
        "rep",
        scatter_dimension=1,
        tiled=True,
    ).astype(jnp.float32)
    outer_grad = summed / lax.axis_size("rep")
    new_momentum = momentum_coef * momentum[0] + outer_grad
    new_master = master[0] - outer_rate * (outer_grad + momentum_coef * new_momentum)
    weight_bf = new_master.astype(jnp.bfloat16)
    local_tokens = tokens[0]
    token_cols = lax.all_to_all(local_tokens, "shard", split_axis=1, concat_axis=0, tiled=True)
    projected = lax.psum_scatter(
        jnp.dot(token_cols, weight_bf, preferred_element_type=jnp.float32).astype(jnp.bfloat16),
        "shard",
        scatter_dimension=0,
        tiled=True,
    )
    return (new_master[None], new_momentum[None], projected[None])


def line_kernel(
    chunk, lag,
    delta_hbm, master_hbm, momentum_hbm, token_hbm,
    new_master_hbm, new_momentum_hbm, probe_hbm,
    theirs, mine, master, momentum, weight, token, probe,
    pair_send, pair_recv, load_sem, store_sem,
    weight_send, weight_recv, pass_send, token_send, token_recv, token_load,
    probe_send, probe_recv, probe_store,
):
    count, rows, _ = theirs.shape
    half = count * chunk
    r = lax.axis_index("rep")
    z = lax.axis_index("shard")
    twin = {"rep": 1 - r}
    mate_at = z + 1 - 2 * lax.rem(z, 2)
    across_at = 3 - z
    mate = {"shard": mate_at}
    across = {"shard": across_at}
    inner = jnp.logical_and(z > 0, z < 3)
    outer = jnp.logical_not(inner)

    def columns(i):
        return pl.ds(pl.multiple_of(i * chunk, chunk), chunk)

    def half_columns(which, i):
        return pl.ds(pl.multiple_of(which * half + i * chunk, chunk), chunk)

    def loads(i):
        return (
            pltpu.make_async_copy(delta_hbm.at[:, half_columns(r, i)], mine.at[i], load_sem.at[0, i]),
            pltpu.make_async_copy(master_hbm.at[:, columns(i)], master.at[i], load_sem.at[1, i]),
            pltpu.make_async_copy(momentum_hbm.at[:, columns(i)], momentum.at[i], load_sem.at[2, i]),
        )

    def pair_copy(i):
        return pltpu.make_async_remote_copy(
            src_ref=delta_hbm.at[:, half_columns(1 - r, i)],
            dst_ref=theirs.at[i],
            send_sem=pair_send,
            recv_sem=pair_recv.at[i],
            device_id=twin,
            device_id_type=MESH,
        )

    def weight_copy(block, i, send_sem, slot, target):
        return pltpu.make_async_remote_copy(
            src_ref=weight.at[block, i],
            dst_ref=weight.at[block, i],
            send_sem=send_sem,
            recv_sem=weight_recv.at[slot, i],
            device_id=target,
            device_id_type=MESH,
        )

    def token_copy():
        return pltpu.make_async_remote_copy(
            src_ref=token_hbm,
            dst_ref=token.at[1],
            send_sem=token_send,
            recv_sem=token_recv,
            device_id=mate,
            device_id_type=MESH,
        )

    def probe_copy(j):
        return pltpu.make_async_remote_copy(
            src_ref=probe.at[1, j],
            dst_ref=probe_hbm.at[:, columns(j)],
            send_sem=probe_send,
            recv_sem=probe_recv,
            device_id=mate,
            device_id_type=MESH,
        )

    barrier = pltpu.get_barrier_semaphore()
    pl.semaphore_signal(barrier, inc=1, device_id=twin, device_id_type=MESH)
    pl.semaphore_signal(barrier, inc=1, device_id=mate, device_id_type=MESH)

    @pl.when(inner)
    def _():
        pl.semaphore_signal(barrier, inc=1, device_id=across, device_id_type=MESH)
        pl.semaphore_wait(barrier, 3)

    @pl.when(outer)
    def _():
        pl.semaphore_wait(barrier, 2)

    @pl.loop(0, AHEAD)
    def _(i):
        pair_copy(i).start()
        for copy in loads(i):
            copy.start()

    @pl.when(outer)
    def _():
        token_copy().start()

    own_tokens = pltpu.make_async_copy(token_hbm, token.at[0], token_load)

    @pl.when(inner)
    def _():
        own_tokens.start()

    @pl.loop(0, count + lag + TRAIL)
    def _(i):
        @pl.when(i + AHEAD < count)
        def _():
            pair_copy(i + AHEAD).start()
            for copy in loads(i + AHEAD):
                copy.start()

        @pl.when(i < count)
        def _():
            for copy in loads(i):
                copy.wait()
            pair_copy(i).wait_recv()
            outer_grad = (mine[i].astype(jnp.float32) + theirs[i].astype(jnp.float32)) * 0.5
            new_momentum = momentum_coef * momentum[i] + outer_grad
            new_master = master[i] - outer_rate * (outer_grad + momentum_coef * new_momentum)
            weight[z, i] = new_master.astype(jnp.bfloat16)
            master[i] = new_master
            momentum[i] = new_momentum

            @pl.when(inner)
            def _():
                weight_copy(z, i, weight_send, 1, across).start()

            @pl.when(outer)
            def _():
                weight_copy(z, i, weight_send, 0, mate).start()

            pltpu.make_async_copy(master.at[i], new_master_hbm.at[:, columns(i)], store_sem.at[0]).start()
            pltpu.make_async_copy(momentum.at[i], new_momentum_hbm.at[:, columns(i)], store_sem.at[1]).start()

        j = i - lag

        @pl.when(jnp.logical_and(inner, jnp.logical_and(j >= 0, j < count)))
        def _():
            weight_copy(mate_at, j, pass_send, 0, across).wait_recv()
            weight_copy(mate_at, j, pass_send, 2, across).start()

        k = i - lag - TRAIL

        @pl.when(jnp.logical_and(inner, k >= 0))
        def _():
            @pl.when(k == 0)
            def _():
                own_tokens.wait()
                token_copy().wait_recv()

            weight_copy(across_at, k, weight_send, 1, across).wait_recv()
            weight_copy(3 - mate_at, k, pass_send, 2, across).wait_recv()
            for owner in range(2):
                @pl.loop(0, rows // ROWS)
                def _(b):
                    span = pl.ds(pl.multiple_of(b * ROWS, ROWS), ROWS)
                    total = jnp.zeros((ROWS, chunk), jnp.float32)
                    for block in range(4):
                        total += jnp.dot(
                            token[owner, span, block * rows:(block + 1) * rows],
                            weight[block, k],
                            preferred_element_type=jnp.float32,
                        )
                    probe[owner, k, span, :] = total.astype(jnp.bfloat16)

            probe_copy(k).start()
            pltpu.make_async_copy(probe.at[0, k], probe_hbm.at[:, columns(k)], probe_store).start()

    pltpu.make_async_copy(theirs, theirs, pair_send).wait()
    pltpu.make_async_copy(weight.at[0], weight.at[0], weight_send).wait()
    pltpu.make_async_copy(master, master, store_sem.at[0]).wait()
    pltpu.make_async_copy(momentum, momentum, store_sem.at[1]).wait()

    @pl.when(inner)
    def _():
        pltpu.make_async_copy(weight.at[0], weight.at[0], pass_send).wait()
        pltpu.make_async_copy(probe.at[0], probe.at[0], probe_send).wait()
        pltpu.make_async_copy(probe.at[0], probe.at[0], probe_store).wait()

    @pl.when(outer)
    def _():
        token_copy().wait_send()
        pltpu.make_async_copy(probe_hbm, probe_hbm, probe_recv).wait()


def line_body(deltas, master, momentum, tokens):
    rows, half = master.shape[1:]
    width = tokens.shape[2]
    count = half // CHUNK
    lag = width // CHUNK
    bf16, f32 = jnp.bfloat16, jnp.float32
    dma = pltpu.SemaphoreType.DMA
    anywhere = pl.BlockSpec(memory_space=pl.ANY)
    new_master, new_momentum, probe = pl.pallas_call(
        functools.partial(line_kernel, CHUNK, lag),
        out_shape=(
            jax.ShapeDtypeStruct((rows, half), f32),
            jax.ShapeDtypeStruct((rows, half), f32),
            jax.ShapeDtypeStruct((rows, half), bf16),
        ),
        in_specs=[anywhere] * 4,
        out_specs=(anywhere,) * 3,
        scratch_shapes=[
            pltpu.VMEM((count, rows, CHUNK), bf16),
            pltpu.VMEM((count, rows, CHUNK), bf16),
            pltpu.VMEM((count, rows, CHUNK), f32),
            pltpu.VMEM((count, rows, CHUNK), f32),
            pltpu.VMEM((4, count, rows, CHUNK), bf16),
            pltpu.VMEM((2, rows, width), bf16),
            pltpu.VMEM((2, count, rows, CHUNK), bf16),
            dma,
            dma((count,)),
            dma((3, count)),
            dma((2,)),
            dma,
            dma((3, count)),
            dma,
            dma,
            dma,
            dma,
            dma,
            dma,
            dma,
        ],
        compiler_params=pltpu.CompilerParams(
            collective_id=0, has_side_effects=True, vmem_limit_bytes=60 * 1024 * 1024
        ),
    )(deltas[0, 0], master[0], momentum[0], tokens[0])
    return (new_master[None], new_momentum[None], probe[None])


def solution(mesh):
    placed = (
        P("rep", "exp", "shard", None),
        P("exp", "shard", "rep"),
        P("exp", "shard", "rep"),
        P("exp", "shard", None),
    )
    paired = mesh.shape["rep"] == 2 and mesh.shape["shard"] == 4
    return jax.shard_map(
        line_body if paired else plain_body,
        mesh=mesh,
        in_specs=placed,
        out_specs=(P("exp", "shard", "rep"), P("exp", "shard", "rep"), P("exp", "shard", "rep")),
        check_vma=False,
    )
```

```python
import functools

import jax
import jax.numpy as jnp
from jax import lax
from jax.experimental import pallas as pl
from jax.experimental.pallas import tpu as pltpu
from jax.sharding import PartitionSpec as P

outer_rate = 0.7
momentum_coef = 0.9
MESH = pl.DeviceIdType.MESH
CHUNK = 128
AHEAD = 6
TRAIL = 3
ROWS = 256


def plain_body(deltas, master, momentum, tokens):
    summed = lax.psum_scatter(
        deltas[0, 0].astype(jnp.float32).astype(jnp.bfloat16),
        "rep",
        scatter_dimension=1,
        tiled=True,
    ).astype(jnp.float32)
    outer_grad = summed / lax.axis_size("rep")
    new_momentum = momentum_coef * momentum[0] + outer_grad
    new_master = master[0] - outer_rate * (outer_grad + momentum_coef * new_momentum)
    weight_bf = new_master.astype(jnp.bfloat16)
    local_tokens = tokens[0]
    token_cols = lax.all_to_all(local_tokens, "shard", split_axis=1, concat_axis=0, tiled=True)
    projected = lax.psum_scatter(
        jnp.dot(token_cols, weight_bf, preferred_element_type=jnp.float32).astype(jnp.bfloat16),
        "shard",
        scatter_dimension=0,
        tiled=True,
    )
    return (new_master[None], new_momentum[None], projected[None])


def line_kernel(
    chunk, lag,
    delta_hbm, master_hbm, momentum_hbm, token_hbm,
    master, momentum, probe,
    theirs, mine, weight, token, mate_probe,
    pair_send, pair_recv, load_sem,
    weight_send, weight_recv, pass_send, token_send, token_recv, token_load,
    probe_send, probe_recv,
):
    count, rows, _ = theirs.shape
    half = count * chunk
    r = lax.axis_index("rep")
    z = lax.axis_index("shard")
    twin = {"rep": 1 - r}
    mate_at = z + 1 - 2 * lax.rem(z, 2)
    across_at = 3 - z
    mate = {"shard": mate_at}
    across = {"shard": across_at}
    inner = jnp.logical_and(z > 0, z < 3)
    outer = jnp.logical_not(inner)

    def columns(i):
        return pl.ds(pl.multiple_of(i * chunk, chunk), chunk)

    def half_columns(which, i):
        return pl.ds(pl.multiple_of(which * half + i * chunk, chunk), chunk)

    def loads(i):
        return (
            pltpu.make_async_copy(delta_hbm.at[:, half_columns(r, i)], mine.at[i], load_sem.at[0, i]),
            pltpu.make_async_copy(master_hbm.at[:, columns(i)], master.at[i], load_sem.at[1, i]),
            pltpu.make_async_copy(momentum_hbm.at[:, columns(i)], momentum.at[i], load_sem.at[2, i]),
        )

    def pair_copy(i):
        return pltpu.make_async_remote_copy(
            src_ref=delta_hbm.at[:, half_columns(1 - r, i)],
            dst_ref=theirs.at[i],
            send_sem=pair_send,
            recv_sem=pair_recv.at[i],
            device_id=twin,
            device_id_type=MESH,
        )

    def weight_copy(block, i, send_sem, slot, target):
        return pltpu.make_async_remote_copy(
            src_ref=weight.at[block, i],
            dst_ref=weight.at[block, i],
            send_sem=send_sem,
            recv_sem=weight_recv.at[slot, i],
            device_id=target,
            device_id_type=MESH,
        )

    def token_copy():
        return pltpu.make_async_remote_copy(
            src_ref=token_hbm,
            dst_ref=token.at[1],
            send_sem=token_send,
            recv_sem=token_recv,
            device_id=mate,
            device_id_type=MESH,
        )

    def probe_copy(j):
        return pltpu.make_async_remote_copy(
            src_ref=mate_probe.at[j],
            dst_ref=probe.at[j],
            send_sem=probe_send,
            recv_sem=probe_recv,
            device_id=mate,
            device_id_type=MESH,
        )

    barrier = pltpu.get_barrier_semaphore()
    pl.semaphore_signal(barrier, inc=1, device_id=twin, device_id_type=MESH)
    pl.semaphore_signal(barrier, inc=1, device_id=mate, device_id_type=MESH)

    @pl.when(inner)
    def _():
        pl.semaphore_signal(barrier, inc=1, device_id=across, device_id_type=MESH)
        pl.semaphore_wait(barrier, 3)

    @pl.when(outer)
    def _():
        pl.semaphore_wait(barrier, 2)

    @pl.loop(0, AHEAD)
    def _(i):
        pair_copy(i).start()
        for copy in loads(i):
            copy.start()

    @pl.when(outer)
    def _():
        token_copy().start()

    own_tokens = pltpu.make_async_copy(token_hbm, token.at[0], token_load)

    @pl.when(inner)
    def _():
        own_tokens.start()

    @pl.loop(0, count + lag + TRAIL)
    def _(i):
        @pl.when(i + AHEAD < count)
        def _():
            pair_copy(i + AHEAD).start()
            for copy in loads(i + AHEAD):
                copy.start()

        @pl.when(i < count)
        def _():
            for copy in loads(i):
                copy.wait()
            pair_copy(i).wait_recv()
            outer_grad = (mine[i].astype(jnp.float32) + theirs[i].astype(jnp.float32)) * 0.5
            new_momentum = momentum_coef * momentum[i] + outer_grad
            new_master = master[i] - outer_rate * (outer_grad + momentum_coef * new_momentum)
            weight[z, i] = new_master.astype(jnp.bfloat16)
            master[i] = new_master
            momentum[i] = new_momentum

            @pl.when(inner)
            def _():
                weight_copy(z, i, weight_send, 1, across).start()

            @pl.when(outer)
            def _():
                weight_copy(z, i, weight_send, 0, mate).start()

        j = i - lag

        @pl.when(jnp.logical_and(inner, jnp.logical_and(j >= 0, j < count)))
        def _():
            weight_copy(mate_at, j, pass_send, 0, across).wait_recv()
            weight_copy(mate_at, j, pass_send, 2, across).start()

        k = i - lag - TRAIL

        @pl.when(jnp.logical_and(inner, k >= 0))
        def _():
            @pl.when(k == 0)
            def _():
                own_tokens.wait()
                token_copy().wait_recv()

            weight_copy(across_at, k, weight_send, 1, across).wait_recv()
            weight_copy(3 - mate_at, k, pass_send, 2, across).wait_recv()
            for owner, result in enumerate((probe, mate_probe)):
                @pl.loop(0, rows // ROWS)
                def _(b):
                    span = pl.ds(pl.multiple_of(b * ROWS, ROWS), ROWS)
                    total = jnp.zeros((ROWS, chunk), jnp.float32)
                    for block in range(4):
                        total += jnp.dot(
                            token[owner, span, block * rows:(block + 1) * rows],
                            weight[block, k],
                            preferred_element_type=jnp.float32,
                        )
                    result[k, span, :] = total.astype(jnp.bfloat16)

            probe_copy(k).start()

    pltpu.make_async_copy(theirs, theirs, pair_send).wait()
    pltpu.make_async_copy(weight.at[0], weight.at[0], weight_send).wait()

    @pl.when(inner)
    def _():
        pltpu.make_async_copy(weight.at[0], weight.at[0], pass_send).wait()
        pltpu.make_async_copy(mate_probe, mate_probe, probe_send).wait()

    @pl.when(outer)
    def _():
        token_copy().wait_send()
        pltpu.make_async_copy(probe, probe, probe_recv).wait()


def store_kernel(chunk, *refs):
    copies = []
    for at in range(3):
        source, target, sem = refs[at], refs[3 + at], refs[6].at[at]
        for i in range(source.shape[0]):
            copies.append(pltpu.make_async_copy(source.at[i], target.at[:, pl.ds(i * chunk, chunk)], sem))
    for copy in copies:
        copy.start()
    for at in range(3):
        pltpu.make_async_copy(refs[at], refs[at], refs[6].at[at]).wait()


def line_body(deltas, master, momentum, tokens):
    rows, half = master.shape[1:]
    width = tokens.shape[2]
    count = half // CHUNK
    lag = width // CHUNK
    bf16, f32 = jnp.bfloat16, jnp.float32
    dma = pltpu.SemaphoreType.DMA
    anywhere = pl.BlockSpec(memory_space=pl.ANY)
    local = pl.BlockSpec(memory_space=pltpu.VMEM)
    blocks = (count, rows, CHUNK)
    results = pl.pallas_call(
        functools.partial(line_kernel, CHUNK, lag),
        out_shape=(pltpu.VMEM(blocks, f32), pltpu.VMEM(blocks, f32), pltpu.VMEM(blocks, bf16)),
        in_specs=[anywhere] * 4,
        out_specs=(local,) * 3,
        scratch_shapes=[
            pltpu.VMEM(blocks, bf16),
            pltpu.VMEM(blocks, bf16),
            pltpu.VMEM((4,) + blocks, bf16),
            pltpu.VMEM((2, rows, width), bf16),
            pltpu.VMEM(blocks, bf16),
            dma,
            dma((count,)),
            dma((3, count)),
            dma,
            dma((3, count)),
            dma,
            dma,
            dma,
            dma,
            dma,
            dma,
        ],
        compiler_params=pltpu.CompilerParams(
            collective_id=0, has_side_effects=True, vmem_limit_bytes=45 * 1024 * 1024
        ),
    )(deltas[0, 0], master[0], momentum[0], tokens[0])
    new_master, new_momentum, probe = pl.pallas_call(
        functools.partial(store_kernel, CHUNK),
        out_shape=(
            jax.ShapeDtypeStruct((rows, half), f32),
            jax.ShapeDtypeStruct((rows, half), f32),
            jax.ShapeDtypeStruct((rows, half), bf16),
        ),
        in_specs=[local] * 3,
        out_specs=(anywhere,) * 3,
        scratch_shapes=[dma((3,))],
        compiler_params=pltpu.CompilerParams(vmem_limit_bytes=1024 * 1024),
    )(*results)
    return (new_master[None], new_momentum[None], probe[None])


def solution(mesh):
    placed = (
        P("rep", "exp", "shard", None),
        P("exp", "shard", "rep"),
        P("exp", "shard", "rep"),
        P("exp", "shard", None),
    )
    paired = mesh.shape["rep"] == 2 and mesh.shape["shard"] == 4
    return jax.shard_map(
        line_body if paired else plain_body,
        mesh=mesh,
        in_specs=placed,
        out_specs=(P("exp", "shard", "rep"), P("exp", "shard", "rep"), P("exp", "shard", "rep")),
        check_vma=False,
    )
```

```python
import functools

import jax
import jax.numpy as jnp
from jax import lax
from jax.experimental import pallas as pl
from jax.experimental.pallas import tpu as pltpu
from jax.sharding import PartitionSpec as P

outer_rate = 0.7
momentum_coef = 0.9
MESH = pl.DeviceIdType.MESH
CHUNK = 128
AHEAD = 6
EARLY = 3
TRAIL = 6
ROWS = 256


def plain_body(deltas, master, momentum, tokens):
    summed = lax.psum_scatter(
        deltas[0, 0].astype(jnp.float32).astype(jnp.bfloat16),
        "rep",
        scatter_dimension=1,
        tiled=True,
    ).astype(jnp.float32)
    outer_grad = summed / lax.axis_size("rep")
    new_momentum = momentum_coef * momentum[0] + outer_grad
    new_master = master[0] - outer_rate * (outer_grad + momentum_coef * new_momentum)
    weight_bf = new_master.astype(jnp.bfloat16)
    local_tokens = tokens[0]
    token_cols = lax.all_to_all(local_tokens, "shard", split_axis=1, concat_axis=0, tiled=True)
    projected = lax.psum_scatter(
        jnp.dot(token_cols, weight_bf, preferred_element_type=jnp.float32).astype(jnp.bfloat16),
        "shard",
        scatter_dimension=0,
        tiled=True,
    )
    return (new_master[None], new_momentum[None], projected[None])


def line_kernel(
    chunk, lag,
    delta_hbm, master_hbm, momentum_hbm, token_hbm,
    master, momentum, probe,
    theirs, mine, weight, token, mate_probe,
    pair_send, pair_recv, load_sem,
    weight_send, weight_recv, pass_send, token_send, token_recv, token_load,
    probe_send, probe_recv,
):
    count, rows, _ = theirs.shape
    half = count * chunk
    r = lax.axis_index("rep")
    z = lax.axis_index("shard")
    twin = {"rep": 1 - r}
    mate_at = z + 1 - 2 * lax.rem(z, 2)
    across_at = 3 - z
    mate = {"shard": mate_at}
    across = {"shard": across_at}
    inner = jnp.logical_and(z > 0, z < 3)
    outer = jnp.logical_not(inner)

    def columns(i):
        return pl.ds(pl.multiple_of(i * chunk, chunk), chunk)

    def half_columns(which, i):
        return pl.ds(pl.multiple_of(which * half + i * chunk, chunk), chunk)

    def loads(i):
        return (
            pltpu.make_async_copy(delta_hbm.at[:, half_columns(r, i)], mine.at[i], load_sem.at[0, i]),
            pltpu.make_async_copy(master_hbm.at[:, columns(i)], master.at[i], load_sem.at[1, i]),
            pltpu.make_async_copy(momentum_hbm.at[:, columns(i)], momentum.at[i], load_sem.at[2, i]),
        )

    def pair_copy(i):
        return pltpu.make_async_remote_copy(
            src_ref=delta_hbm.at[:, half_columns(1 - r, i)],
            dst_ref=theirs.at[i],
            send_sem=pair_send,
            recv_sem=pair_recv.at[i],
            device_id=twin,
            device_id_type=MESH,
        )

    def weight_copy(block, i, send_sem, slot, target):
        return pltpu.make_async_remote_copy(
            src_ref=weight.at[block, i],
            dst_ref=weight.at[block, i],
            send_sem=send_sem,
            recv_sem=weight_recv.at[slot, i],
            device_id=target,
            device_id_type=MESH,
        )

    def token_copy():
        return pltpu.make_async_remote_copy(
            src_ref=token_hbm,
            dst_ref=token.at[1],
            send_sem=token_send,
            recv_sem=token_recv,
            device_id=mate,
            device_id_type=MESH,
        )

    def probe_copy(j):
        return pltpu.make_async_remote_copy(
            src_ref=mate_probe.at[j],
            dst_ref=probe.at[j],
            send_sem=probe_send,
            recv_sem=probe_recv,
            device_id=mate,
            device_id_type=MESH,
        )

    barrier = pltpu.get_barrier_semaphore()
    pl.semaphore_signal(barrier, inc=1, device_id=twin, device_id_type=MESH)
    pl.semaphore_signal(barrier, inc=1, device_id=mate, device_id_type=MESH)

    @pl.when(inner)
    def _():
        pl.semaphore_signal(barrier, inc=1, device_id=across, device_id_type=MESH)
        pl.semaphore_wait(barrier, 3)

    @pl.when(outer)
    def _():
        pl.semaphore_wait(barrier, 2)

    @pl.loop(0, AHEAD)
    def _(i):
        pair_copy(i).start()
        for copy in loads(i):
            copy.start()

    own_tokens = pltpu.make_async_copy(token_hbm, token.at[0], token_load)

    @pl.when(inner)
    def _():
        own_tokens.start()

    @pl.loop(0, count + lag + TRAIL)
    def _(i):
        @pl.when(i + AHEAD < count)
        def _():
            pair_copy(i + AHEAD).start()
            for copy in loads(i + AHEAD):
                copy.start()

        @pl.when(i < count)
        def _():
            for copy in loads(i):
                copy.wait()
            pair_copy(i).wait_recv()
            outer_grad = (mine[i].astype(jnp.float32) + theirs[i].astype(jnp.float32)) * 0.5
            new_momentum = momentum_coef * momentum[i] + outer_grad
            new_master = master[i] - outer_rate * (outer_grad + momentum_coef * new_momentum)
            weight[z, i] = new_master.astype(jnp.bfloat16)
            master[i] = new_master
            momentum[i] = new_momentum

            @pl.when(inner)
            def _():
                weight_copy(z, i, weight_send, 1, across).start()

            @pl.when(outer)
            def _():
                weight_copy(z, i, weight_send, 0, mate).start()

                @pl.when(i == EARLY - 1)
                def _():
                    token_copy().start()

        early = i < EARLY + 3
        j = jnp.where(early, i - 3, i - lag)

        @pl.when(jnp.logical_and(inner, jnp.logical_and(j >= jnp.where(early, 0, EARLY), j < count)))
        def _():
            weight_copy(mate_at, j, pass_send, 0, across).wait_recv()
            weight_copy(mate_at, j, pass_send, 2, across).start()

        k = i - lag - TRAIL

        @pl.when(jnp.logical_and(inner, k >= 0))
        def _():
            @pl.when(k == 0)
            def _():
                own_tokens.wait()
                token_copy().wait_recv()

            weight_copy(across_at, k, weight_send, 1, across).wait_recv()
            weight_copy(3 - mate_at, k, pass_send, 2, across).wait_recv()
            def project(owner, result):
                @pl.loop(0, rows // ROWS)
                def _(b):
                    span = pl.ds(pl.multiple_of(b * ROWS, ROWS), ROWS)
                    total = jnp.zeros((ROWS, chunk), jnp.float32)
                    for block in range(4):
                        total += jnp.dot(
                            token[owner, span, block * rows:(block + 1) * rows],
                            weight[block, k],
                            preferred_element_type=jnp.float32,
                        )
                    result[k, span, :] = total.astype(jnp.bfloat16)

            project(1, mate_probe)
            probe_copy(k).start()
            project(0, probe)

    pltpu.make_async_copy(theirs, theirs, pair_send).wait()
    pltpu.make_async_copy(weight.at[0], weight.at[0], weight_send).wait()

    @pl.when(inner)
    def _():
        pltpu.make_async_copy(weight.at[0], weight.at[0], pass_send).wait()
        pltpu.make_async_copy(mate_probe, mate_probe, probe_send).wait()

    @pl.when(outer)
    def _():
        token_copy().wait_send()
        pltpu.make_async_copy(probe, probe, probe_recv).wait()


def store_kernel(chunk, *refs):
    copies = []
    for at in range(3):
        source, target, sem = refs[at], refs[3 + at], refs[6].at[at]
        for i in range(source.shape[0]):
            copies.append(pltpu.make_async_copy(source.at[i], target.at[:, pl.ds(i * chunk, chunk)], sem))
    for copy in copies:
        copy.start()
    for at in range(3):
        pltpu.make_async_copy(refs[at], refs[at], refs[6].at[at]).wait()


def line_body(deltas, master, momentum, tokens):
    rows, half = master.shape[1:]
    width = tokens.shape[2]
    count = half // CHUNK
    lag = width // CHUNK
    bf16, f32 = jnp.bfloat16, jnp.float32
    dma = pltpu.SemaphoreType.DMA
    anywhere = pl.BlockSpec(memory_space=pl.ANY)
    local = pl.BlockSpec(memory_space=pltpu.VMEM)
    blocks = (count, rows, CHUNK)
    results = pl.pallas_call(
        functools.partial(line_kernel, CHUNK, lag),
        out_shape=(pltpu.VMEM(blocks, f32), pltpu.VMEM(blocks, f32), pltpu.VMEM(blocks, bf16)),
        in_specs=[anywhere] * 4,
        out_specs=(local,) * 3,
        scratch_shapes=[
            pltpu.VMEM(blocks, bf16),
            pltpu.VMEM(blocks, bf16),
            pltpu.VMEM((4,) + blocks, bf16),
            pltpu.VMEM((2, rows, width), bf16),
            pltpu.VMEM(blocks, bf16),
            dma,
            dma((count,)),
            dma((3, count)),
            dma,
            dma((3, count)),
            dma,
            dma,
            dma,
            dma,
            dma,
            dma,
        ],
        compiler_params=pltpu.CompilerParams(
            collective_id=0, has_side_effects=True, vmem_limit_bytes=45 * 1024 * 1024
        ),
    )(deltas[0, 0], master[0], momentum[0], tokens[0])
    new_master, new_momentum, probe = pl.pallas_call(
        functools.partial(store_kernel, CHUNK),
        out_shape=(
            jax.ShapeDtypeStruct((rows, half), f32),
            jax.ShapeDtypeStruct((rows, half), f32),
            jax.ShapeDtypeStruct((rows, half), bf16),
        ),
        in_specs=[local] * 3,
        out_specs=(anywhere,) * 3,
        scratch_shapes=[dma((3,))],
        compiler_params=pltpu.CompilerParams(vmem_limit_bytes=1024 * 1024),
    )(*results)
    return (new_master[None], new_momentum[None], probe[None])


def solution(mesh):
    placed = (
        P("rep", "exp", "shard", None),
        P("exp", "shard", "rep"),
        P("exp", "shard", "rep"),
        P("exp", "shard", None),
    )
    paired = mesh.shape["rep"] == 2 and mesh.shape["shard"] == 4
    return jax.shard_map(
        line_body if paired else plain_body,
        mesh=mesh,
        in_specs=placed,
        out_specs=(P("exp", "shard", "rep"), P("exp", "shard", "rep"), P("exp", "shard", "rep")),
        check_vma=False,
    )
```
